32 devices in a mesh: blk: 16 (over z, x, core), rep: 2 (over y).
Axes of the slice: x: 2, y: 2, z: 4, core: 2. Of those that a mesh axis runs over, the one named last changes fastest.
Arguments:
- frames: bfloat16 [2, 768, 384], P('rep', 'blk'), may hold values from -600 to 600
- codebook: bfloat16 [16384, 384], P('blk'), may hold values from -2 to 2
Outputs:
- log_total: float32 [2, 768], P('rep', 'blk')
- counts: float32 [16384], P('blk')
- entropy: float32 [], replicated
The draws below stay inside these ranges and needn't reach their ends.
All inputs are finite; a program needn't handle non-finite values.
Results may differ from the reference program's by a relative error of at most 0.00065.
Values may be sent and summed in bfloat16 or wider, within the bound.
A program may use at most 128 MiB of HBM per device.

```python
import math
import jax
import jax.numpy as jnp
from jax import lax

D = 384
V_DEV = 1024
GROUPS = 2
FR_GROUP = 768
FRAMES = 1536
CODEBOOK = 16384
N_BLK = 16


def draw_codebook(key, part):
    rough_key, value_key = jax.random.split(jax.random.fold_in(key, 23))
    ladder = jnp.arange(CODEBOOK, dtype=jnp.float32) / CODEBOOK
    ramp = 0.6 * jnp.exp(ladder * math.log(3.0))
    rough = jnp.exp(jax.random.uniform(rough_key, (CODEBOOK,), jnp.float32, math.log(0.7), math.log(1.4)))
    values = jax.random.truncated_normal(value_key, -4.0, 4.0, (CODEBOOK, D), jnp.float32)
    scaled = values * (ramp * rough)[:, None] / math.sqrt(D)
    return scaled.astype(jnp.bfloat16)


def draw_frames(key, part):
    keys = jax.random.split(jax.random.fold_in(key, 11), 2)
    row_scale = jnp.exp(jax.random.uniform(keys[0], (GROUPS, FR_GROUP, 1), jnp.float32, math.log(0.3), math.log(3.0)))
    values = jax.random.truncated_normal(keys[1], -4.0, 4.0, (GROUPS, FR_GROUP, D), jnp.float32)
    result = values * row_scale
    return result.astype(jnp.bfloat16)


def setup_inputs(seed: int = 0) -> dict:
    splits = jax.random.split(jax.random.key(seed), 3)
    frames = draw_frames(jax.random.fold_in(splits[2], 71), 0)
    codebook = draw_codebook(jax.random.fold_in(splits[2], 71), 0)
    return dict(frames=frames, codebook=codebook)


def shard_scores(frame_rows, weights):
    return lax.dot_general(frame_rows, weights, (((1,), (1,)), ((), ())), preferred_element_type=jnp.float32)


def group_pass(frame_rows, codebook):
    shards = codebook.reshape(N_BLK, V_DEV, D)

    def stat_step(carried, weights):
        high, total = carried
        scores = shard_scores(frame_rows, weights)
        new_high = jnp.maximum(high, jnp.max(scores, axis=1))
        new_total = total * jnp.exp(high - new_high) + jnp.sum(jnp.exp(scores - new_high[:, None]), axis=1)
        return (new_high, new_total), None

    start_high = jnp.full((FR_GROUP,), -jnp.inf, jnp.float32)
    start_total = jnp.zeros((FR_GROUP,), jnp.float32)
    (row_high, row_total), _ = lax.scan(stat_step, (start_high, start_total), shards)
    row_lse = row_high + jnp.log(row_total)

    def shard_usage(weights):
        scores = shard_scores(frame_rows, weights)
        return jnp.sum(jnp.exp(scores - row_lse[:, None]), axis=0)

    usage = lax.map(shard_usage, shards).reshape(CODEBOOK)
    return row_lse, usage


def reference(frames, codebook):
    lse_list = []
    usage_total = jnp.zeros((CODEBOOK,), jnp.float32)
    for member in range(GROUPS):
        row_lse, usage = group_pass(frames[member], codebook)
        lse_list.append(row_lse)
        usage_total = usage_total + usage
    mean_use = usage_total / FRAMES
    entropy = -jnp.sum(mean_use * jnp.log(mean_use + 1e-7))
    return jnp.stack(lse_list, axis=0), usage_total, entropy
```

```python
import functools

import jax
import jax.numpy as jnp
from jax import lax
from jax.experimental import pallas as pl
from jax.experimental.pallas import tpu as pltpu
from jax.sharding import PartitionSpec as P

MESH = pl.DeviceIdType.MESH
LANES = 128
TILES = 4


def each(count, body):
    if count <= 16:
        for i in range(count):
            body(i)
    else:

        def step(i, carry):
            body(i)
            return carry

        lax.fori_loop(0, count, step, 0)


def kernel(
    n,
    reps,
    frame_ref,
    code_hbm,
    lse_ref,
    use_ref,
    ent_ref,
    code,
    fr,
    exps,
    high,
    stats,
    uses,
    terms,
    code_sem,
    fr_send,
    fr_recv,
    st_send,
    st_recv,
    us_send,
    us_recv,
    te_send,
    te_recv,
):
    depth_z = n // 4
    half = n // 2
    block = frame_ref.shape[1]
    protos = code.shape[0]
    vt = protos // TILES
    width = stats.shape[-1]
    lw = 384 if width % 384 == 0 else width
    groups = width // lw
    me = lax.axis_index("blk")
    rep = lax.axis_index("rep")
    c = me % 2
    x = (me // 2) % 2
    z = me // 4

    def dev(zz, xx, cc):
        return (zz * 2 + xx) * 2 + cc

    def pos(xx, cc, zz):
        return xx * half + cc * depth_z + zz

    def rows(p):
        return pl.ds(pl.multiple_of(p * block, block), block)

    upper = z // (depth_z // 2)
    mirrored = z + upper * (depth_z - 1 - 2 * z)

    def near(j):
        jj = j + (depth_z + j - mirrored) // depth_z
        return jj + upper * (depth_z - 1 - 2 * jj)

    load = pltpu.make_async_copy(code_hbm, code, code_sem)
    load.start()

    barrier = pltpu.get_barrier_semaphore()

    def greet(k):
        pl.semaphore_signal(
            barrier, inc=1, device_id={"blk": (me + k + 1) % n}, device_id_type=MESH
        )

    def greet_rep(k):
        pl.semaphore_signal(
            barrier, inc=1, device_id={"rep": (rep + k + 1) % reps}, device_id_type=MESH
        )

    each(n - 1, greet)
    each(reps - 1, greet_rep)
    pl.semaphore_wait(barrier, n - 1 + reps - 1)

    def frame_copy(src, p, target, slot):
        return pltpu.make_async_remote_copy(
            src_ref=src,
            dst_ref=fr.at[rows(p)],
            send_sem=fr_send.at[slot],
            recv_sem=fr_recv.at[p],
            device_id={"blk": target},
            device_id_type=MESH,
        )

    own = pos(x, c, z)
    mine = frame_ref.at[0]
    x_peer = dev(z, 1 - x, c)
    c_peer = dev(z, x, 1 - c)
    to_z, to_x, to_c = 0, depth_z, 2 * depth_z

    each(depth_z - 1, lambda j: frame_copy(mine, own, dev(near(j), x, c), to_z + j).start())
    frame_copy(mine, own, x_peer, to_x).start()
    frame_copy(mine, own, c_peer, to_c).start()
    fr[rows(own), :] = frame_ref[0]

    def arrived(p):
        frame_copy(fr.at[rows(p)], p, me, 0).wait_recv()

    def relay(j):
        p = pos(x, c, near(j))
        arrived(p)
        frame_copy(fr.at[rows(p)], p, x_peer, to_x + 1 + j).start()
        frame_copy(fr.at[rows(p)], p, c_peer, to_c + 1 + j).start()

    each(depth_z - 1, relay)
    each(depth_z, lambda j: arrived(pos(x, 1 - c, j)))
    load.wait()

    def by_group(body):
        if groups == 1:
            body(0)
        else:

            def step(g, carry):
                body(g * lw)
                return carry

            lax.fori_loop(0, groups, step, 0)

    def score(ch, side, t):
        def body(start):
            first = side * (half * block) + start
            moving = fr[pl.ds(pl.multiple_of(first, block), lw), :]
            s = lax.dot_general(
                code[t * vt : (t + 1) * vt, :],
                moving,
                (((1,), (1,)), ((), ())),
                preferred_element_type=jnp.float32,
            )
            at = pl.ds(start, lw) if groups == 1 else pl.ds(pl.multiple_of(start, LANES), lw)
            exps[ch, t * vt : (t + 1) * vt, at] = s
            top = jnp.max(s.reshape(vt // 8, 8, lw), axis=0)
            high[ch, :, at] = top if t == 0 else jnp.maximum(high[ch, :, at], top)

        by_group(body)

    def soften(ch, side):
        def body(start):
            at = pl.ds(start, lw) if groups == 1 else pl.ds(pl.multiple_of(start, LANES), lw)
            top = jnp.max(high[ch, :, at], axis=0, keepdims=True)
            total = jnp.zeros((8, lw), jnp.float32)
            for t in range(TILES):
                e = jnp.exp(exps[ch, t * vt : (t + 1) * vt, at] - top)
                exps[ch, t * vt : (t + 1) * vt, at] = e
                total = total + jnp.sum(e.reshape(vt // 8, 8, lw), axis=0)
            high[ch, 0:1, at] = top
            stats[me, side, :, at] = top + jnp.log(jnp.sum(total, axis=0, keepdims=True))

        by_group(body)

    def stat_copy(ch, side, source, target, k):
        return pltpu.make_async_remote_copy(
            src_ref=stats.at[source, side],
            dst_ref=stats.at[source, side],
            send_sem=st_send.at[ch, k],
            recv_sem=st_recv.at[source, side],
            device_id={"blk": target},
            device_id_type=MESH,
        )

    def tell(ch, side):
        each(n - 1, lambda k: stat_copy(ch, side, me, (me + k + 1) % n, k).start())

    other = 1 - x
    per_tile = depth_z // TILES

    def relay_x(j):
        p = pos(other, c, z) if isinstance(j, int) and j == 0 else pos(other, c, near(j - 1))
        arrived(p)
        frame_copy(fr.at[rows(p)], p, c_peer, to_c + depth_z + j).start()

    for t in range(TILES):
        score(0, x, t)
        for j in range(t * per_tile, (t + 1) * per_tile):
            relay_x(j)
    soften(0, x)
    tell(0, x)

    each(depth_z, lambda j: arrived(pos(other, 1 - c, j)))
    for t in range(TILES):
        score(1, other, t)
    soften(1, other)
    tell(1, other)

    def merged(side, at):
        parts = stats[:, side, :, at]
        top = jnp.max(parts, axis=0)
        return top + jnp.log(jnp.sum(jnp.exp(parts - top[None]), axis=0))

    folded = [None] * TILES
    for ch, side in ((0, x), (1, other)):
        each(n - 1, lambda k: stat_copy(ch, side, (me + k + 1) % n, me, 0).wait_recv())
        for g in range(groups):
            at = pl.ds(g * lw, lw)
            lse = merged(side, at)
            if ch == 0:
                high[0, 1:2, at] = lse
            w = jnp.exp(high[ch, 0:1, at] - lse)
            for t in range(TILES):
                for q in range(lw // LANES):
                    cols = pl.ds(g * lw + q * LANES, LANES)
                    term = exps[ch, t * vt : (t + 1) * vt, cols] * w[:, q * LANES : (q + 1) * LANES]
                    folded[t] = term if folded[t] is None else folded[t] + term

    ones = jnp.ones((8, LANES), jnp.float32)
    for t in range(TILES):
        part = lax.dot_general(
            ones,
            folded[t],
            (((1,), (1,)), ((), ())),
            precision=lax.Precision.HIGHEST,
            preferred_element_type=jnp.float32,
        )
        uses[rep, :, t * vt : (t + 1) * vt] = part[0:1, :]

    def use_copy(source, target, k):
        return pltpu.make_async_remote_copy(
            src_ref=uses.at[source],
            dst_ref=uses.at[source],
            send_sem=us_send.at[k],
            recv_sem=us_recv.at[source],
            device_id={"rep": target},
            device_id_type=MESH,
        )

    each(reps - 1, lambda k: use_copy(rep, (rep + k + 1) % reps, k).start())

    shift = (c * depth_z + z) * block
    row = jnp.broadcast_to(high[0, 1:2, :], (8, width))
    lse_ref[...] = pltpu.roll(row, (width - shift) % width, 1)[0:1, 0:block]

    each(reps - 1, lambda k: use_copy((rep + k + 1) % reps, rep, k).wait_recv())
    usage = uses[0]
    for k in range(1, reps):
        usage = usage + uses[k]
    use_ref[...] = usage
    mean_use = usage / jnp.float32(n * block * reps)
    term = -jnp.sum(mean_use * jnp.log(mean_use + 1e-07), axis=1, keepdims=True)
    terms[me] = jnp.broadcast_to(term, (1, LANES))

    def term_copy(source, target, k):
        return pltpu.make_async_remote_copy(
            src_ref=terms.at[source],
            dst_ref=terms.at[source],
            send_sem=te_send.at[k],
            recv_sem=te_recv.at[source],
            device_id={"blk": target},
            device_id_type=MESH,
        )

    each(n - 1, lambda k: term_copy(me, (me + k + 1) % n, k).start())

    each(depth_z - 1, lambda s: frame_copy(mine, own, me, to_z + s).wait_send())
    each(3 * depth_z, lambda s: frame_copy(mine, own, me, to_x + s).wait_send())
    for ch, side in ((0, x), (1, other)):
        each(n - 1, lambda k: stat_copy(ch, side, me, me, k).wait_send())
    each(reps - 1, lambda k: use_copy(rep, rep, k).wait_send())

    each(n - 1, lambda k: term_copy((me + k + 1) % n, me, 0).wait_recv())
    ent_ref[0, 0] = jnp.sum(terms[...], axis=0)[0, 0]
    each(n - 1, lambda k: term_copy(me, me, k).wait_send())


def per_device(n, reps, frames, codebook):
    block = frames.shape[1]
    protos, depth = codebook.shape
    width = n // 2 * block
    dz = n // 4
    dma = pltpu.SemaphoreType.DMA
    lse, usage, entropy = pl.pallas_call(
        functools.partial(kernel, n, reps),
        out_shape=(
            jax.ShapeDtypeStruct((1, block), jnp.float32),
            jax.ShapeDtypeStruct((1, protos), jnp.float32),
            jax.ShapeDtypeStruct((1, 1), jnp.float32),
        ),
        in_specs=[
            pl.BlockSpec(memory_space=pltpu.VMEM),
            pl.BlockSpec(memory_space=pl.ANY),
        ],
        out_specs=(
            pl.BlockSpec(memory_space=pltpu.VMEM),
            pl.BlockSpec(memory_space=pltpu.VMEM),
            pl.BlockSpec(memory_space=pltpu.SMEM),
        ),
        scratch_shapes=[
            pltpu.VMEM((protos, depth), jnp.bfloat16),
            pltpu.VMEM((n * block, depth), jnp.bfloat16),
            pltpu.VMEM((2, protos, width), jnp.float32),
            pltpu.VMEM((2, 8, width), jnp.float32),
            pltpu.VMEM((n, 2, 1, width), jnp.float32),
            pltpu.VMEM((reps, 1, protos), jnp.float32),
            pltpu.VMEM((n, 1, LANES), jnp.float32),
            dma,
            dma((4 * dz,)),
            dma((n,)),
            dma((2, n)),
            dma((n, 2)),
            dma((reps,)),
            dma((reps,)),
            dma((n,)),
            dma((n,)),
        ],
        compiler_params=pltpu.CompilerParams(collective_id=0, has_side_effects=True),
    )(frames, codebook)
    return lse, usage.reshape(protos), entropy.reshape(())


def solution(mesh):
    sizes = dict(mesh.shape)
    return jax.shard_map(
        functools.partial(per_device, sizes["blk"], sizes["rep"]),
        mesh=mesh,
        in_specs=(P("rep", "blk", None), P("blk", None)),
        out_specs=(P("rep", "blk"), P("blk"), P()),
        check_vma=False,
    )
```

```python
import functools

import jax
import jax.numpy as jnp
from jax import lax
from jax.experimental import pallas as pl
from jax.experimental.pallas import tpu as pltpu
from jax.sharding import PartitionSpec as P

MESH = pl.DeviceIdType.MESH
LANES = 128
VT = 256


def each(count, body):
    if count <= 16:
        for i in range(count):
            body(i)
    else:

        def step(i, carry):
            body(i)
            return carry

        lax.fori_loop(0, count, step, 0)


def kernel(
    n,
    reps,
    frame_hbm,
    code_hbm,
    lse_ref,
    use_ref,
    ent_ref,
    code,
    fr,
    exps,
    high,
    stats,
    uses,
    terms,
    code_sem,
    own_sem,
    code_send,
    code_recv,
    fr_send,
    fr_recv,
    st_send,
    st_recv,
    us_send,
    us_recv,
    te_send,
    te_recv,
):
    deep = n // 4
    half = n // 2
    block = frame_hbm.shape[1]
    protos = code.shape[1]
    tiles = protos // VT
    width = stats.shape[-1]
    used = deep * block
    lw = 256 if width % 256 == 0 else width
    groups = width // lw
    me = lax.axis_index("blk")
    rep = lax.axis_index("rep")
    c = me % 2
    x = (me // 2) % 2
    z = me // 4
    q_me = x * deep + z
    other = 1 - x

    def dev(zz, xx, cc):
        return (zz * 2 + xx) * 2 + cc

    def dev_q(q):
        return dev(q % deep, q // deep, c)

    def rows(zz):
        return pl.ds(pl.multiple_of(zz * block, block), block)

    upper = z // (deep // 2)
    mirrored = z + upper * (deep - 1 - 2 * z)

    def near(j):
        jj = j + (deep + j - mirrored) // deep
        return jj + upper * (deep - 1 - 2 * jj)

    x_peer = dev(z, other, c)
    c_peer = dev(z, x, 1 - c)

    barrier = pltpu.get_barrier_semaphore()

    def greet(**where):
        pl.semaphore_signal(barrier, inc=1, device_id=where, device_id_type=MESH)

    each(deep - 1, lambda j: greet(blk=dev(near(j), x, c)))
    greet(blk=x_peer)
    greet(blk=c_peer)
    for k in range(1, reps):
        greet(rep=(rep + k) % reps, blk=me)
        greet(rep=(rep + k) % reps, blk=c_peer)
    own = pltpu.make_async_copy(frame_hbm.at[0], fr.at[x, rows(z)], own_sem)
    own.start()
    load = pltpu.make_async_copy(code_hbm, code.at[c], code_sem)
    load.start()
    if width > used:
        fr[:, used:, :] = jnp.zeros((2, width - used, fr.shape[2]), fr.dtype)
    own.wait()
    pl.semaphore_wait(barrier, deep + 1 + 2 * (reps - 1))

    def frame_copy(xx, zz, target, slot):
        return pltpu.make_async_remote_copy(
            src_ref=fr.at[xx, rows(zz)],
            dst_ref=fr.at[xx, rows(zz)],
            send_sem=fr_send.at[slot],
            recv_sem=fr_recv.at[xx, zz],
            device_id={"blk": target},
            device_id_type=MESH,
        )

    def code_copy(cc, target):
        return pltpu.make_async_remote_copy(
            src_ref=code_hbm,
            dst_ref=code.at[cc],
            send_sem=code_send,
            recv_sem=code_recv,
            device_id={"blk": target},
            device_id_type=MESH,
        )

    each(deep - 1, lambda j: frame_copy(x, z, dev(near(j), x, c), j).start())
    frame_copy(x, z, x_peer, deep).start()
    code_copy(c, c_peer).start()

    def arrived(xx, zz):
        frame_copy(xx, zz, x_peer, 0).wait_recv()

    def relay(j):
        arrived(x, near(j))
        frame_copy(x, near(j), x_peer, deep + 1 + j).start()

    each(deep - 1, relay)

    def by_group(body):
        if groups == 1:
            body(pl.ds(0, lw))
        else:

            def step(g, carry):
                body(pl.ds(pl.multiple_of(g * lw, lw), lw))
                return carry

            lax.fori_loop(0, groups, step, 0)

    def score(ch, side, cc, first):
        def body(at):
            moving = fr[side, at, :]
            top = None
            for t in range(tiles):
                s = lax.dot_general(
                    code[cc, t * VT : (t + 1) * VT, :],
                    moving,
                    (((1,), (1,)), ((), ())),
                    preferred_element_type=jnp.float32,
                )
                exps[ch, cc, t * VT : (t + 1) * VT, at] = s
                peak = jnp.max(s.reshape(VT // 8, 8, lw), axis=0)
                top = peak if top is None else jnp.maximum(top, peak)
            high[ch, :, at] = top if first else jnp.maximum(high[ch, :, at], top)

        by_group(body)

    def soften(ch, side):
        def body(at):
            top = jnp.max(high[ch, :, at], axis=0, keepdims=True)
            total = jnp.zeros((8, lw), jnp.float32)
            for cc in range(2):
                for t in range(tiles):
                    e = jnp.exp(exps[ch, cc, t * VT : (t + 1) * VT, at] - top)
                    exps[ch, cc, t * VT : (t + 1) * VT, at] = e
                    total = total + jnp.sum(e.reshape(VT // 8, 8, lw), axis=0)
            high[ch, 0:1, at] = top
            stats[q_me, side, :, at] = top + jnp.log(jnp.sum(total, axis=0, keepdims=True))

        by_group(body)

    def stat_copy(ch, side, source, target, k):
        return pltpu.make_async_remote_copy(
            src_ref=stats.at[source, side],
            dst_ref=stats.at[source, side],
            send_sem=st_send.at[ch, k],
            recv_sem=st_recv.at[source, side],
            device_id={"blk": target},
            device_id_type=MESH,
        )

    def peer(k):
        return (q_me + k + 1) % half

    def tell(ch, side):
        each(half - 1, lambda k: stat_copy(ch, side, q_me, dev_q(peer(k)), k).start())

    load.wait()
    score(0, x, c, True)
    code_copy(1 - c, c_peer).wait_recv()
    score(0, x, 1 - c, False)
    soften(0, x)
    each(deep, lambda j: arrived(other, j))
    tell(0, x)
    score(1, other, 0, True)
    score(1, other, 1, False)
    soften(1, other)
    tell(1, other)

    def merged(side, at):
        parts = stats[:, side, :, at]
        top = jnp.max(parts, axis=0)
        return top + jnp.log(jnp.sum(jnp.exp(parts - top[None]), axis=0))

    folded = [None] * (2 * tiles)
    for ch, side in ((0, x), (1, other)):
        each(half - 1, lambda k: stat_copy(ch, side, peer(k), x_peer, 0).wait_recv())
        for g in range(groups):
            at = pl.ds(g * lw, lw)
            lse = merged(side, at)
            if ch == 0:
                high[0, 1:2, at] = lse
            w = jnp.exp(high[ch, 0:1, at] - lse)
            if width > used:
                lane = lax.broadcasted_iota(jnp.int32, (1, lw), 1) + g * lw
                w = jnp.where(lane < used, w, 0.0)
            for t in range(2 * tiles):
                for q in range(lw // LANES):
                    e = exps[
                        ch,
                        t // tiles,
                        t % tiles * VT : (t % tiles + 1) * VT,
                        pl.ds(g * lw + q * LANES, LANES),
                    ]
                    part = e * w[:, q * LANES : (q + 1) * LANES]
                    folded[t] = part if folded[t] is None else folded[t] + part

    ones = jnp.ones((8, LANES), jnp.float32)
    here = rep * 2 + c
    for t in range(2 * tiles):
        part = lax.dot_general(
            ones,
            folded[t],
            (((1,), (1,)), ((), ())),
            precision=lax.Precision.HIGHEST,
            preferred_element_type=jnp.float32,
        )
        uses[here, t // tiles, :, t % tiles * VT : (t % tiles + 1) * VT] = part[0:1, :]

    def use_copy(source, target_rep, target, k):
        return pltpu.make_async_remote_copy(
            src_ref=uses.at[source],
            dst_ref=uses.at[source],
            send_sem=us_send.at[k],
            recv_sem=us_recv.at[source],
            device_id={"rep": target_rep, "blk": target},
            device_id_type=MESH,
        )

    for k in range(1, reps):
        to = (rep + k) % reps
        use_copy(here, to, me, 2 * k).start()
        use_copy(here, to, c_peer, 2 * k + 1).start()
    use_copy(here, rep, c_peer, 1).start()

    row = jnp.broadcast_to(high[0, 1:2, :], (8, width))
    lse_ref[...] = pltpu.roll(row, (width - z * block) % width, 1)[0:1, 0:block]

    for k in range(1, 2 * reps):
        use_copy((here + k) % (2 * reps), rep, c_peer, 0).wait_recv()
    usage = uses[0]
    for k in range(1, 2 * reps):
        usage = usage + uses[k]
    uses_own = uses[0, c]
    for k in range(1, 2 * reps):
        uses_own = uses_own + uses[k, c]
    use_ref[...] = uses_own
    mean_use = usage / jnp.float32(n * block * reps)
    term = mean_use * jnp.log(mean_use + 1e-07)
    term = -jnp.sum(term[0] + term[1], axis=1, keepdims=True)
    terms[q_me] = jnp.broadcast_to(term, (1, LANES))

    def term_copy(source, target, k):
        return pltpu.make_async_remote_copy(
            src_ref=terms.at[source],
            dst_ref=terms.at[source],
            send_sem=te_send.at[k],
            recv_sem=te_recv.at[source],
            device_id={"blk": target},
            device_id_type=MESH,
        )

    each(half - 1, lambda k: term_copy(q_me, dev_q(peer(k)), k).start())

    each(deep - 1, lambda s: frame_copy(x, z, x_peer, s).wait_send())
    each(deep, lambda s: frame_copy(x, z, x_peer, deep + s).wait_send())
    code_copy(c, c_peer).wait_send()
    for ch, side in ((0, x), (1, other)):
        each(half - 1, lambda k: stat_copy(ch, side, q_me, x_peer, k).wait_send())
    for k in range(1, 2 * reps):
        use_copy(here, rep, c_peer, k).wait_send()

    each(half - 1, lambda k: term_copy(peer(k), x_peer, 0).wait_recv())
    ent_ref[0, 0] = jnp.sum(terms[...], axis=0)[0, 0]
    each(half - 1, lambda k: term_copy(q_me, x_peer, k).wait_send())


def per_device(n, reps, frames, codebook):
    block = frames.shape[1]
    protos, depth = codebook.shape
    deep, half = n // 4, n // 2
    width = -(-deep * block // LANES) * LANES
    dma = pltpu.SemaphoreType.DMA
    lse, usage, entropy = pl.pallas_call(
        functools.partial(kernel, n, reps),
        out_shape=(
            OUT((1, block), jnp.float32),
            OUT((1, protos), jnp.float32),
            jax.ShapeDtypeStruct((1, 1), jnp.float32),
        ),
        in_specs=[
            pl.BlockSpec(memory_space=pl.ANY),
            pl.BlockSpec(memory_space=pl.ANY),
        ],
        out_specs=(
            pl.BlockSpec(memory_space=pltpu.VMEM),
            pl.BlockSpec(memory_space=pltpu.VMEM),
            pl.BlockSpec(memory_space=pltpu.SMEM),
        ),
        scratch_shapes=[
            pltpu.VMEM((2, protos, depth), jnp.bfloat16),
            pltpu.VMEM((2, width, depth), jnp.bfloat16),
            pltpu.VMEM((2, 2, protos, width), jnp.float32),
            pltpu.VMEM((2, 8, width), jnp.float32),
            pltpu.VMEM((half, 2, 1, width), jnp.float32),
            pltpu.VMEM((2 * reps, 2, 1, protos), jnp.float32),
            pltpu.VMEM((half, 1, LANES), jnp.float32),
            dma,
            dma,
            dma,
            dma,
            dma((2 * deep,)),
            dma((2, deep)),
            dma((2, half)),
            dma((half, 2)),
            dma((2 * reps,)),
            dma((2 * reps,)),
            dma((half,)),
            dma((half,)),
        ],
        compiler_params=pltpu.CompilerParams(collective_id=0, has_side_effects=True),
    )(frames, codebook)
    return lse, usage.reshape(protos), entropy.reshape(())


OUT = pltpu.VMEM


def solution(mesh):
    sizes = dict(mesh.shape)
    return jax.shard_map(
        functools.partial(per_device, sizes["blk"], sizes["rep"]),
        mesh=mesh,
        in_specs=(P("rep", "blk", None), P("blk", None)),
        out_specs=(P("rep", "blk"), P("blk"), P()),
        check_vma=False,
    )
```

```python
import functools

import jax
import jax.numpy as jnp
from jax import lax
from jax.experimental import pallas as pl
from jax.experimental.pallas import tpu as pltpu
from jax.sharding import PartitionSpec as P

MESH = pl.DeviceIdType.MESH
LANES = 128
VT = 256


def each(count, body):
    if count <= 16:
        for i in range(count):
            body(i)
    else:

        def step(i, carry):
            body(i)
            return carry

        lax.fori_loop(0, count, step, 0)


def kernel(
    n,
    reps,
    frame_hbm,
    code_hbm,
    lse_ref,
    use_ref,
    ent_ref,
    code,
    fr,
    exps,
    high,
    sums,
    row_lse,
    stats,
    uses,
    terms,
    code_sem,
    own_sem,
    code_send,
    code_recv,
    fr_send,
    fr_recv,
    st_send,
    st_recv,
    us_send,
    us_recv,
    te_send,
    te_recv,
):
    deep = n // 4
    half = n // 2
    block = frame_hbm.shape[1]
    protos = code.shape[1]
    tiles = protos // VT
    width = stats.shape[-1]
    used = deep * block
    lw = 256 if width % 256 == 0 else width
    groups = width // lw
    me = lax.axis_index("blk")
    rep = lax.axis_index("rep")
    c = me % 2
    x = (me // 2) % 2
    z = me // 4
    q_me = x * deep + z
    other = 1 - x

    def dev(zz, xx, cc):
        return (zz * 2 + xx) * 2 + cc

    def dev_q(q):
        return dev(q % deep, q // deep, c)

    def rows(zz):
        return pl.ds(pl.multiple_of(zz * block, block), block)

    upper = z // (deep // 2)
    mirrored = z + upper * (deep - 1 - 2 * z)

    def near(j):
        jj = j + (deep + j - mirrored) // deep
        return jj + upper * (deep - 1 - 2 * jj)

    x_peer = dev(z, other, c)
    c_peer = dev(z, x, 1 - c)

    barrier = pltpu.get_barrier_semaphore()

    def greet(**where):
        pl.semaphore_signal(barrier, inc=1, device_id=where, device_id_type=MESH)

    each(deep - 1, lambda j: greet(blk=dev(near(j), x, c)))
    greet(blk=x_peer)
    greet(blk=c_peer)
    for k in range(1, reps):
        greet(rep=(rep + k) % reps, blk=me)
        greet(rep=(rep + k) % reps, blk=c_peer)
    own = pltpu.make_async_copy(frame_hbm.at[0], fr.at[x, rows(z)], own_sem)
    own.start()
    load = pltpu.make_async_copy(code_hbm, code.at[c], code_sem)
    load.start()
    if width > used:
        fr[:, used:, :] = jnp.zeros((2, width - used, fr.shape[2]), fr.dtype)
    own.wait()
    pl.semaphore_wait(barrier, deep + 1 + 2 * (reps - 1))

    def frame_copy(xx, zz, target, slot):
        return pltpu.make_async_remote_copy(
            src_ref=fr.at[xx, rows(zz)],
            dst_ref=fr.at[xx, rows(zz)],
            send_sem=fr_send.at[slot],
            recv_sem=fr_recv.at[xx, zz],
            device_id={"blk": target},
            device_id_type=MESH,
        )

    def code_copy(cc, target):
        return pltpu.make_async_remote_copy(
            src_ref=code_hbm,
            dst_ref=code.at[cc],
            send_sem=code_send,
            recv_sem=code_recv,
            device_id={"blk": target},
            device_id_type=MESH,
        )

    frame_copy(x, z, x_peer, deep).start()
    each(deep - 1, lambda j: frame_copy(x, z, dev(near(deep - 2 - j), x, c), j).start())
    code_copy(c, c_peer).start()

    def arrived(xx, zz):
        frame_copy(xx, zz, x_peer, 0).wait_recv()

    def relay(j):
        arrived(x, near(j))
        frame_copy(x, near(j), x_peer, deep + 1 + j).start()

    each(deep - 1, relay)

    def by_group(body):
        if groups == 1:
            body(pl.ds(0, lw))
        else:

            def step(g, carry):
                body(pl.ds(pl.multiple_of(g * lw, lw), lw))
                return carry

            lax.fori_loop(0, groups, step, 0)

    def score(ch, side, cc):
        def body(at):
            moving = fr[side, at, :]
            for t in range(tiles):
                row = cc * tiles + t
                s = lax.dot_general(
                    code[cc, t * VT : (t + 1) * VT, :],
                    moving,
                    (((1,), (1,)), ((), ())),
                    preferred_element_type=jnp.float32,
                )
                peak = jnp.max(s, axis=0, keepdims=True)
                e = jnp.exp(s - peak)
                exps[ch, cc, t * VT : (t + 1) * VT, at] = e
                high[ch, pl.ds(row, 1), at] = peak
                sums[ch, pl.ds(row, 1), at] = jnp.sum(e, axis=0, keepdims=True)

        by_group(body)

    def soften(ch, side):
        def body(at):
            peaks = high[ch, :, at]
            top = jnp.max(peaks, axis=0, keepdims=True)
            total = jnp.sum(sums[ch, :, at] * jnp.exp(peaks - top), axis=0, keepdims=True)
            stats[q_me, side, :, at] = top + jnp.log(total)

        by_group(body)

    def stat_copy(ch, side, source, target, k):
        return pltpu.make_async_remote_copy(
            src_ref=stats.at[source, side],
            dst_ref=stats.at[source, side],
            send_sem=st_send.at[ch, k],
            recv_sem=st_recv.at[source, side],
            device_id={"blk": target},
            device_id_type=MESH,
        )

    def peer(k):
        return (q_me + k + 1) % half

    def tell(ch, side):
        each(half - 1, lambda k: stat_copy(ch, side, q_me, dev_q(peer(k)), k).start())

    load.wait()
    score(0, x, c)
    code_copy(1 - c, c_peer).wait_recv()
    score(0, x, 1 - c)
    soften(0, x)
    each(deep, lambda j: arrived(other, j))
    tell(0, x)
    score(1, other, 0)
    score(1, other, 1)
    soften(1, other)
    tell(1, other)

    def merged(side, at):
        parts = stats[:, side, :, at]
        top = jnp.max(parts, axis=0)
        return top + jnp.log(jnp.sum(jnp.exp(parts - top[None]), axis=0))

    folded = [None] * (2 * tiles)
    for ch, side in ((0, x), (1, other)):
        each(half - 1, lambda k: stat_copy(ch, side, peer(k), x_peer, 0).wait_recv())
        for g in range(groups):
            at = pl.ds(g * lw, lw)
            lse = merged(side, at)
            if ch == 0:
                row_lse[:, at] = lse
            w = jnp.exp(high[ch, :, at] - lse)
            if width > used:
                lane = lax.broadcasted_iota(jnp.int32, (1, lw), 1) + g * lw
                w = jnp.where(lane < used, w, 0.0)
            for t in range(2 * tiles):
                for q in range(lw // LANES):
                    e = exps[
                        ch,
                        t // tiles,
                        t % tiles * VT : (t % tiles + 1) * VT,
                        pl.ds(g * lw + q * LANES, LANES),
                    ]
                    part = e * w[t : t + 1, q * LANES : (q + 1) * LANES]
                    folded[t] = part if folded[t] is None else folded[t] + part

    ones = jnp.ones((8, 3 * LANES), jnp.bfloat16)
    here = rep * 2 + c
    for t in range(2 * tiles):
        big = folded[t].astype(jnp.bfloat16)
        rest = folded[t] - big.astype(jnp.float32)
        mid = rest.astype(jnp.bfloat16)
        low = (rest - mid.astype(jnp.float32)).astype(jnp.bfloat16)
        part = lax.dot_general(
            ones,
            jnp.concatenate([big, mid, low], axis=1),
            (((1,), (1,)), ((), ())),
            preferred_element_type=jnp.float32,
        )
        uses[here, t // tiles, :, t % tiles * VT : (t % tiles + 1) * VT] = part[0:1, :]

    def use_copy(source, target_rep, target, k):
        return pltpu.make_async_remote_copy(
            src_ref=uses.at[source],
            dst_ref=uses.at[source],
            send_sem=us_send.at[k],
            recv_sem=us_recv.at[source],
            device_id={"rep": target_rep, "blk": target},
            device_id_type=MESH,
        )

    for k in range(1, reps):
        to = (rep + k) % reps
        use_copy(here, to, me, 2 * k).start()
        use_copy(here, to, c_peer, 2 * k + 1).start()
    use_copy(here, rep, c_peer, 1).start()

    row = jnp.broadcast_to(row_lse[...], (8, width))
    lse_ref[...] = pltpu.roll(row, (width - z * block) % width, 1)[0:1, 0:block]

    for k in range(1, 2 * reps):
        use_copy((here + k) % (2 * reps), rep, c_peer, 0).wait_recv()
    usage = uses[0]
    for k in range(1, 2 * reps):
        usage = usage + uses[k]
    uses_own = uses[0, c]
    for k in range(1, 2 * reps):
        uses_own = uses_own + uses[k, c]
    use_ref[...] = uses_own
    mean_use = usage / jnp.float32(n * block * reps)
    term = mean_use * jnp.log(mean_use + 1e-07)
    term = -jnp.sum(term[0] + term[1], axis=1, keepdims=True)
    terms[q_me] = jnp.broadcast_to(term, (1, LANES))

    def term_copy(source, target, k):
        return pltpu.make_async_remote_copy(
            src_ref=terms.at[source],
            dst_ref=terms.at[source],
            send_sem=te_send.at[k],
            recv_sem=te_recv.at[source],
            device_id={"blk": target},
            device_id_type=MESH,
        )

    each(half - 1, lambda k: term_copy(q_me, dev_q(peer(k)), k).start())

    each(deep - 1, lambda s: frame_copy(x, z, x_peer, s).wait_send())
    each(deep, lambda s: frame_copy(x, z, x_peer, deep + s).wait_send())
    code_copy(c, c_peer).wait_send()
    for ch, side in ((0, x), (1, other)):
        each(half - 1, lambda k: stat_copy(ch, side, q_me, x_peer, k).wait_send())
    for k in range(1, 2 * reps):
        use_copy(here, rep, c_peer, k).wait_send()

    each(half - 1, lambda k: term_copy(peer(k), x_peer, 0).wait_recv())
    ent_ref[0, 0] = jnp.sum(terms[...], axis=0)[0, 0]
    each(half - 1, lambda k: term_copy(q_me, x_peer, k).wait_send())


def per_device(n, reps, frames, codebook):
    block = frames.shape[1]
    protos, depth = codebook.shape
    deep, half = n // 4, n // 2
    width = -(-deep * block // LANES) * LANES
    dma = pltpu.SemaphoreType.DMA
    lse, usage, entropy = pl.pallas_call(
        functools.partial(kernel, n, reps),
        out_shape=(
            OUT((1, block), jnp.float32),
            OUT((1, protos), jnp.float32),
            jax.ShapeDtypeStruct((1, 1), jnp.float32),
        ),
        in_specs=[
            pl.BlockSpec(memory_space=pl.ANY),
            pl.BlockSpec(memory_space=pl.ANY),
        ],
        out_specs=(
            pl.BlockSpec(memory_space=pltpu.VMEM),
            pl.BlockSpec(memory_space=pltpu.VMEM),
            pl.BlockSpec(memory_space=pltpu.SMEM),
        ),
        scratch_shapes=[
            pltpu.VMEM((2, protos, depth), jnp.bfloat16),
            pltpu.VMEM((2, width, depth), jnp.bfloat16),
            pltpu.VMEM((2, 2, protos, width), jnp.float32),
            pltpu.VMEM((2, 2 * (protos // VT), width), jnp.float32),
            pltpu.VMEM((2, 2 * (protos // VT), width), jnp.float32),
            pltpu.VMEM((1, width), jnp.float32),
            pltpu.VMEM((half, 2, 1, width), jnp.float32),
            pltpu.VMEM((2 * reps, 2, 1, protos), jnp.float32),
            pltpu.VMEM((half, 1, LANES), jnp.float32),
            dma,
            dma,
            dma,
            dma,
            dma((2 * deep,)),
            dma((2, deep)),
            dma((2, half)),
            dma((half, 2)),
            dma((2 * reps,)),
            dma((2 * reps,)),
            dma((half,)),
            dma((half,)),
        ],
        compiler_params=pltpu.CompilerParams(collective_id=0, has_side_effects=True),
    )(frames, codebook)
    return lse, usage.reshape(protos), entropy.reshape(())


OUT = pltpu.VMEM


def solution(mesh):
    sizes = dict(mesh.shape)
    return jax.shard_map(
        functools.partial(per_device, sizes["blk"], sizes["rep"]),
        mesh=mesh,
        in_specs=(P("rep", "blk", None), P("blk", None)),
        out_specs=(P("rep", "blk"), P("blk"), P()),
        check_vma=False,
    )
```

```python
import functools

import jax
import jax.numpy as jnp
from jax import lax
from jax.experimental import pallas as pl
from jax.experimental.pallas import tpu as pltpu
from jax.sharding import PartitionSpec as P

MESH = pl.DeviceIdType.MESH
LANES = 128
VT = 256


def each(count, body):
    if count <= 16:
        for i in range(count):
            body(i)
    else:

        def step(i, carry):
            body(i)
            return carry

        lax.fori_loop(0, count, step, 0)


def kernel(
    n,
    reps,
    frame_hbm,
    code_hbm,
    lse_ref,
    use_ref,
    ent_ref,
    code,
    fr,
    exps,
    high,
    sums,
    row_lse,
    stats,
    uses,
    terms,
    code_sem,
    own_sem,
    code_send,
    code_recv,
    fr_send,
    fr_recv,
    st_send,
    st_recv,
    us_send,
    us_recv,
    te_send,
    te_recv,
    up_ready,
):
    deep = n // 4
    half = n // 2
    block = frame_hbm.shape[1]
    protos = code.shape[1]
    tiles = protos // VT
    width = stats.shape[-1]
    used = deep * block
    lw = 256 if width % 256 == 0 else width
    groups = width // lw
    me = lax.axis_index("blk")
    rep = lax.axis_index("rep")
    c = me % 2
    x = (me // 2) % 2
    z = me // 4
    q_me = x * deep + z
    other = 1 - x

    def dev(zz, xx, cc):
        return (zz * 2 + xx) * 2 + cc

    def dev_q(q):
        return dev(q % deep, q // deep, c)

    def rows(zz):
        return pl.ds(pl.multiple_of(zz * block, block), block)

    x_peer = dev(z, other, c)
    c_peer = dev(z, x, 1 - c)

    barrier = pltpu.get_barrier_semaphore()

    def greet(**where):
        pl.semaphore_signal(barrier, inc=1, device_id=where, device_id_type=MESH)

    def above(j, body):
        pl.when(z + 1 + j < deep)(lambda: body(z + 1 + j))

    def below(j, body):
        pl.when(j < z)(lambda: body(z - 1 - j))

    each(deep - 1, lambda j: above(j, lambda zz: greet(blk=dev(zz, x, c))))
    greet(blk=x_peer)
    greet(blk=c_peer)
    for k in range(1, reps):
        greet(rep=(rep + k) % reps, blk=me)
        greet(rep=(rep + k) % reps, blk=c_peer)
    own = pltpu.make_async_copy(frame_hbm.at[0], fr.at[x, rows(z)], own_sem)
    own.start()
    load = pltpu.make_async_copy(code_hbm, code.at[c], code_sem)
    load.start()
    if width > used:
        fr[:, used:, :] = jnp.zeros((2, width - used, fr.shape[2]), fr.dtype)
    own.wait()
    pl.semaphore_wait(barrier, z + 2 + 2 * (reps - 1))

    def ready(zz):
        pl.semaphore_signal(
            up_ready.at[z], inc=1, device_id={"blk": dev(zz, x, c)}, device_id_type=MESH
        )

    each(deep - 1, lambda j: pl.when(j < z)(lambda: ready(j)))

    def frame_copy(xx, zz, target, way, slot):
        return pltpu.make_async_remote_copy(
            src_ref=fr.at[xx, rows(zz)],
            dst_ref=fr.at[xx, rows(zz)],
            send_sem=fr_send.at[way, slot],
            recv_sem=fr_recv.at[xx, zz],
            device_id={"blk": target},
            device_id_type=MESH,
        )

    def code_copy(cc, target):
        return pltpu.make_async_remote_copy(
            src_ref=code_hbm,
            dst_ref=code.at[cc],
            send_sem=code_send,
            recv_sem=code_recv,
            device_id={"blk": target},
            device_id_type=MESH,
        )

    each(deep - 1, lambda j: pl.when(j < z)(lambda: frame_copy(x, z, dev(j, x, c), 0, j).start()))
    frame_copy(x, z, x_peer, 1, z).start()
    code_copy(c, c_peer).start()

    def arrived(xx, zz):
        frame_copy(xx, zz, x_peer, 0, 0).wait_recv()

    def relay(zz):
        arrived(x, zz)
        frame_copy(x, zz, x_peer, 1, zz).start()

    def send_up(zz):
        pl.semaphore_wait(up_ready.at[zz], 1)
        frame_copy(x, z, dev(zz, x, c), 0, zz).start()

    above(0, send_up)
    above(1, send_up)
    each(deep - 1, lambda j: below(j, relay))

    def onward(j):
        above(j, relay)
        above(j + 2, send_up)

    each(deep - 1, onward)

    def by_group(body):
        if groups == 1:
            body(pl.ds(0, lw))
        else:

            def step(g, carry):
                body(pl.ds(pl.multiple_of(g * lw, lw), lw))
                return carry

            lax.fori_loop(0, groups, step, 0)

    def score(ch, side, cc):
        def body(at):
            moving = fr[side, at, :]
            for t in range(tiles):
                row = cc * tiles + t
                s = lax.dot_general(
                    code[cc, t * VT : (t + 1) * VT, :],
                    moving,
                    (((1,), (1,)), ((), ())),
                    preferred_element_type=jnp.float32,
                )
                peak = jnp.max(s, axis=0, keepdims=True)
                e = jnp.exp(s - peak)
                exps[ch, cc, t * VT : (t + 1) * VT, at] = e
                high[ch, pl.ds(row, 1), at] = peak
                sums[ch, pl.ds(row, 1), at] = jnp.sum(e, axis=0, keepdims=True)

        by_group(body)

    def soften(ch, side):
        def body(at):
            peaks = high[ch, :, at]
            top = jnp.max(peaks, axis=0, keepdims=True)
            total = jnp.sum(sums[ch, :, at] * jnp.exp(peaks - top), axis=0, keepdims=True)
            stats[q_me, side, :, at] = top + jnp.log(total)

        by_group(body)

    def stat_copy(ch, side, source, target, k):
        return pltpu.make_async_remote_copy(
            src_ref=stats.at[source, side],
            dst_ref=stats.at[source, side],
            send_sem=st_send.at[ch, k],
            recv_sem=st_recv.at[source, side],
            device_id={"blk": target},
            device_id_type=MESH,
        )

    def peer(k):
        return (q_me + k + 1) % half

    def tell(ch, side):
        each(half - 1, lambda k: stat_copy(ch, side, q_me, dev_q(peer(k)), k).start())

    load.wait()
    score(0, x, c)
    code_copy(1 - c, c_peer).wait_recv()
    score(0, x, 1 - c)
    soften(0, x)
    each(deep, lambda j: arrived(other, j))
    tell(0, x)
    score(1, other, 0)
    score(1, other, 1)
    soften(1, other)
    tell(1, other)

    def merged(side, at):
        parts = stats[:, side, :, at]
        top = jnp.max(parts, axis=0)
        return top + jnp.log(jnp.sum(jnp.exp(parts - top[None]), axis=0))

    folded = [None] * (2 * tiles)
    for ch, side in ((0, x), (1, other)):
        each(half - 1, lambda k: stat_copy(ch, side, peer(k), x_peer, 0).wait_recv())
        for g in range(groups):
            at = pl.ds(g * lw, lw)
            lse = merged(side, at)
            if ch == 0:
                row_lse[:, at] = lse
            w = jnp.exp(high[ch, :, at] - lse)
            if width > used:
                lane = lax.broadcasted_iota(jnp.int32, (1, lw), 1) + g * lw
                w = jnp.where(lane < used, w, 0.0)
            for t in range(2 * tiles):
                for q in range(lw // LANES):
                    e = exps[
                        ch,
                        t // tiles,
                        t % tiles * VT : (t % tiles + 1) * VT,
                        pl.ds(g * lw + q * LANES, LANES),
                    ]
                    part = e * w[t : t + 1, q * LANES : (q + 1) * LANES]
                    folded[t] = part if folded[t] is None else folded[t] + part

    ones = jnp.ones((8, 3 * LANES), jnp.bfloat16)
    here = rep * 2 + c
    for t in range(2 * tiles):
        big = folded[t].astype(jnp.bfloat16)
        rest = folded[t] - big.astype(jnp.float32)
        mid = rest.astype(jnp.bfloat16)
        low = (rest - mid.astype(jnp.float32)).astype(jnp.bfloat16)
        part = lax.dot_general(
            ones,
            jnp.concatenate([big, mid, low], axis=1),
            (((1,), (1,)), ((), ())),
            preferred_element_type=jnp.float32,
        )
        uses[here, t // tiles, :, t % tiles * VT : (t % tiles + 1) * VT] = part[0:1, :]

    def use_copy(source, target_rep, target, k):
        return pltpu.make_async_remote_copy(
            src_ref=uses.at[source],
            dst_ref=uses.at[source],
            send_sem=us_send.at[k],
            recv_sem=us_recv.at[source],
            device_id={"rep": target_rep, "blk": target},
            device_id_type=MESH,
        )

    for k in range(1, reps):
        to = (rep + k) % reps
        use_copy(here, to, me, 2 * k).start()
        use_copy(here, to, c_peer, 2 * k + 1).start()
    use_copy(here, rep, c_peer, 1).start()

    row = jnp.broadcast_to(row_lse[...], (8, width))
    lse_ref[...] = pltpu.roll(row, (width - z * block) % width, 1)[0:1, 0:block]

    for k in range(1, 2 * reps):
        use_copy((here + k) % (2 * reps), rep, c_peer, 0).wait_recv()
    usage = uses[0]
    for k in range(1, 2 * reps):
        usage = usage + uses[k]
    uses_own = uses[0, c]
    for k in range(1, 2 * reps):
        uses_own = uses_own + uses[k, c]
    use_ref[...] = uses_own
    mean_use = usage / jnp.float32(n * block * reps)
    term = mean_use * jnp.log(mean_use + 1e-07)
    term = -jnp.sum(term[0] + term[1], axis=1, keepdims=True)
    terms[q_me] = jnp.broadcast_to(term, (1, LANES))

    def term_copy(source, target, k):
        return pltpu.make_async_remote_copy(
            src_ref=terms.at[source],
            dst_ref=terms.at[source],
            send_sem=te_send.at[k],
            recv_sem=te_recv.at[source],
            device_id={"blk": target},
            device_id_type=MESH,
        )

    each(half - 1, lambda k: term_copy(q_me, dev_q(peer(k)), k).start())

    each(deep - 1, lambda j: below(j, lambda s: frame_copy(x, z, x_peer, 0, s).wait_send()))
    each(deep - 1, lambda j: above(j, lambda s: frame_copy(x, z, x_peer, 0, s).wait_send()))
    each(deep, lambda s: frame_copy(x, z, x_peer, 1, s).wait_send())
    code_copy(c, c_peer).wait_send()
    for ch, side in ((0, x), (1, other)):
        each(half - 1, lambda k: stat_copy(ch, side, q_me, x_peer, k).wait_send())
    for k in range(1, 2 * reps):
        use_copy(here, rep, c_peer, k).wait_send()

    each(half - 1, lambda k: term_copy(peer(k), x_peer, 0).wait_recv())
    ent_ref[0, 0] = jnp.sum(terms[...], axis=0)[0, 0]
    each(half - 1, lambda k: term_copy(q_me, x_peer, k).wait_send())


def per_device(n, reps, frames, codebook):
    block = frames.shape[1]
    protos, depth = codebook.shape
    deep, half = n // 4, n // 2
    width = -(-deep * block // LANES) * LANES
    dma = pltpu.SemaphoreType.DMA
    lse, usage, entropy = pl.pallas_call(
        functools.partial(kernel, n, reps),
        out_shape=(
            OUT((1, block), jnp.float32),
            OUT((1, protos), jnp.float32),
            jax.ShapeDtypeStruct((1, 1), jnp.float32),
        ),
        in_specs=[
            pl.BlockSpec(memory_space=pl.ANY),
            pl.BlockSpec(memory_space=pl.ANY),
        ],
        out_specs=(
            pl.BlockSpec(memory_space=pltpu.VMEM),
            pl.BlockSpec(memory_space=pltpu.VMEM),
            pl.BlockSpec(memory_space=pltpu.SMEM),
        ),
        scratch_shapes=[
            pltpu.VMEM((2, protos, depth), jnp.bfloat16),
            pltpu.VMEM((2, width, depth), jnp.bfloat16),
            pltpu.VMEM((2, 2, protos, width), jnp.float32),
            pltpu.VMEM((2, 2 * (protos // VT), width), jnp.float32),
            pltpu.VMEM((2, 2 * (protos // VT), width), jnp.float32),
            pltpu.VMEM((1, width), jnp.float32),
            pltpu.VMEM((half, 2, 1, width), jnp.float32),
            pltpu.VMEM((2 * reps, 2, 1, protos), jnp.float32),
            pltpu.VMEM((half, 1, LANES), jnp.float32),
            dma,
            dma,
            dma,
            dma,
            dma((2, deep)),
            dma((2, deep)),
            dma((2, half)),
            dma((half, 2)),
            dma((2 * reps,)),
            dma((2 * reps,)),
            dma((half,)),
            dma((half,)),
            pltpu.SemaphoreType.REGULAR((deep,)),
        ],
        compiler_params=pltpu.CompilerParams(collective_id=0, has_side_effects=True),
    )(frames, codebook)
    return lse, usage.reshape(protos), entropy.reshape(())


OUT = pltpu.VMEM


def solution(mesh):
    sizes = dict(mesh.shape)
    return jax.shard_map(
        functools.partial(per_device, sizes["blk"], sizes["rep"]),
        mesh=mesh,
        in_specs=(P("rep", "blk", None), P("blk", None)),
        out_specs=(P("rep", "blk"), P("blk"), P()),
        check_vma=False,
    )
```
